32 devices in a mesh: tm: 8 (over z, core), expert: 4 (over y, x).
Axes of the slice: x: 2, y: 2, z: 4, core: 2. Of those that a mesh axis runs over, the one named last changes fastest.
Arguments:
- tokens: bfloat16 [4, 8, 128, 2048], P('expert', 'tm'), may hold values from -29 to 29
- queries: bfloat16 [4, 8, 128, 2048], P('expert', 'tm'), may hold values from -40 to 40
- key_rows: bfloat16 [4, 8, 128, 2048], P('expert', 'tm'), may hold values from -7 to 7
- values: bfloat16 [4, 8, 128, 2048], P('expert', 'tm'), may hold values from -18 to 18
- actions: int32 [4, 8], P('expert', 'tm'), may hold values from 0 to 63
- action_table: bfloat16 [64, 2048], replicated, may hold values from -6 to 6
- norm_gain: float32 [2048], replicated, may hold values from 0.5 to 1.5
- routes: int32 [4, 8, 128, 2], P('expert', 'tm'), may hold values from 0 to 3, all different within a row; in each aligned block of 128 rows (0 to 127, 128 to 255, ..., all dimensions but the last counted through in order) at most 80 rows name the same one
- gate_probs: float32 [4, 8, 128, 2], P('expert', 'tm'), may hold values from 0.1 to 1
- predicted: int32 [4, 8, 128], P('expert', 'tm'), may hold values 0 or 1
- cotangent: bfloat16 [4, 8, 128, 2048], P('expert', 'tm'), may hold values from -0.8984375 to 0.8984375
- up_weight: bfloat16 [4, 2048, 1024], P('expert'), may hold values from -0.125 to 0.125
- down_weight: bfloat16 [4, 1024, 2048], P('expert'), may hold values from -0.1875 to 0.1875
Outputs:
- layer_out: bfloat16 [4, 8, 128, 2048], P('expert', 'tm')
- stream_grad: bfloat16 [4, 8, 128, 2048], P('expert', 'tm')
- up_grad: bfloat16 [4, 2048, 1024], P('expert', 'tm')
- down_grad: bfloat16 [4, 1024, 2048], P('expert', 'tm')
The draws below stay inside these ranges and needn't reach their ends.
Inputs may be any that keep to these rules, and one draw needn't show every extreme that they name: `routes`: in the 128 tokens of one frame of one clip the 2 experts of a token differ, no expert is named more than 80 times, a bound that some block reaches.
All inputs are finite; a program needn't handle non-finite values. No bound on the sum of `predicted` on one device may be relied on, other than what follows from the above.
Results may differ from the reference program's by a relative error of at most 0.018.
Values may be sent and summed in bfloat16 or wider, within the bound.
No kernel may reach another device: no remote copies, remote signals or barrier semaphores. Data moves between devices by JAX's collectives and lax.ppermute only.
A program may use at most 128 MiB of HBM per device.

```python
import math
import jax
import jax.numpy as jnp
import numpy as np
from jax import lax

D = 2048
HEADS = 16
HD = 128
FF = 1024
ACTIONS = 64
TOPK = 2
FTOK = 128
FRAMES = 8
CLIPS = 4
EXPERTS = 4
CAP = 80


def query_key_pair(key):
    base = jax.random.fold_in(key, 31)
    first, second = jax.random.split(base, 2)
    full_shape = (CLIPS, FRAMES, FTOK, D)
    key_draw = jnp.clip(jax.random.normal(second, full_shape, jnp.float32), -6.0, 6.0)
    query_draw = 2.0 * jnp.clip(jax.random.normal(first, full_shape, jnp.float32), -6.0, 6.0)
    return (query_draw, key_draw)


def draw_queries(key, part):
    return query_key_pair(key)[0].astype(jnp.bfloat16)


def draw_key_rows(key, part):
    return query_key_pair(key)[1].astype(jnp.bfloat16)


def draw_tokens(key, part):
    base = jax.random.fold_in(key, 11)
    first, second = jax.random.split(base, 2)
    full_shape = (CLIPS, FRAMES, FTOK, D)
    column_scale = jnp.exp(jax.random.uniform(second, (D,), jnp.float32, -1.2, 1.2))
    return (jnp.clip(jax.random.normal(first, full_shape, jnp.float32), -6.0, 6.0) * column_scale).astype(jnp.bfloat16)


def with_ends(result, stream_key, least, top_value):
    index_at = [jax.random.randint(jax.random.fold_in(stream_key, axis), (), 0, length) for axis, length in enumerate(result.shape)]
    widest = result.shape.index(max(result.shape))
    beside = index_at[:widest] + [(index_at[widest] + 1) % result.shape[widest]] + index_at[widest + 1:]
    return result.at[tuple(index_at)].set(least).at[tuple(beside)].set(top_value)


def block_scale(key, shape, pieces, low, largest):
    def one(dim, parts):
        heights = jax.random.uniform(jax.random.fold_in(jax.random.fold_in(key, 6), dim), (parts,), jnp.float32, low / len(pieces), largest / len(pieces))
        return jnp.repeat(jnp.exp(heights), shape[dim] // parts).reshape((-1,) + (1,) * (len(shape) - dim - 1))

    loudness = one(*pieces[0])
    for cut in pieces[1:]:
        loudness = loudness * one(*cut)
    return loudness


def routed_block(key, own, number, rows, amount, top, limit, lean):
    ranking = jax.random.permutation(key, amount)
    packed, common = shares(amount, rows * top, limit, lean, True), shares(amount, rows * top, limit, lean, False)
    places = jnp.arange(amount)

    def named(sizes, turn):
        used = int((sizes > 0).sum())
        fixed = max(1, used // 4)
        shifted = fixed + (places - fixed + turn * (used - fixed)) % max(1, amount - fixed)
        return jnp.zeros((amount,), jnp.int32).at[ranking[jnp.where(places < fixed, places, shifted)]].set(jnp.asarray(sizes, jnp.int32))

    sizes = jnp.where(number % 4 == 0, named(packed, number // 4), named(common, number - number // 4 - 1))
    mixed = jax.random.permutation(jax.random.fold_in(own, 3), amount)
    donor, receiver = mixed[0:amount // 2 * 2:2], mixed[1:amount // 2 * 2:2]
    slack = jnp.minimum(sizes[donor] - 1, limit - sizes[receiver]) // 2
    slack = jnp.where((donor == ranking[0]) | (receiver == ranking[0]) | (sizes[receiver] == 0), 0, jnp.maximum(slack, 0))
    shifted = jax.random.randint(jax.random.fold_in(own, 4), (amount // 2,), 0, 1 << 20) % (slack + 1)
    sizes = sizes.at[donor].add(-shifted).at[receiver].add(shifted)
    members = jnp.searchsorted(jnp.cumsum(sizes), jnp.arange(rows * top), side="right").astype(jnp.int32)
    grid = members.reshape(top, rows).T
    grid = grid[jax.random.permutation(jax.random.fold_in(own, 1), rows)]
    turn = jax.random.randint(jax.random.fold_in(own, 2), (rows, 1), 0, top)
    return jnp.take_along_axis(grid, (jnp.arange(top)[None, :] + turn) % top, axis=1)


def shares(number_of, total, most, lean, full):
    loads = [(1 << 20) // math.isqrt(grade ** lean) + 1 for grade in range(1, number_of + 1)]
    largest = most if full else min(most, max(-(-total // number_of), total * loads[0] // sum(loads)))
    least = 1 if total - largest >= number_of - 1 else 0
    given, rest = [largest] + [least] * (number_of - 1), total - largest - least * (number_of - 1)
    while rest > 0:
        candidates = [i for i in range(1, number_of) if given[i] < largest] or [i for i in range(1, number_of) if given[i] < most]
        pool, budget = sum([loads[i] for i in candidates]), rest
        for i in candidates:
            addition = min(most - given[i], max(1, budget * loads[i] // pool), rest)
            given[i] = given[i] + addition
            rest = rest - addition
    return np.array(given)


def bell_draw(key, shape, deviation, reach, cuts=(), held_as=jnp.bfloat16):
    drawn = jax.random.normal(key, shape, jnp.float32) * deviation
    if len(cuts) > 0:
        drawn = block_scale(key, shape, cuts, -0.22, 0.18) * drawn
    return jnp.clip(drawn, min=-reach, max=reach).astype(held_as)


def setup_inputs(seed: int = 0) -> dict:
    splits = jax.random.split(jax.random.key(seed), 14)
    tokens = draw_tokens(jax.random.fold_in(splits[13], 71), 0)
    queries = draw_queries(jax.random.fold_in(splits[13], 71), 0)
    key_rows = draw_key_rows(jax.random.fold_in(splits[13], 71), 0)
    values = bell_draw(splits[3], (CLIPS, FRAMES, FTOK, D), 3.0, 18.0, ((0, 4), (1, 8)))
    actions = with_ends(jax.random.randint(splits[4], (CLIPS, FRAMES), 0, ACTIONS), jax.random.fold_in(splits[4], 1), 0, ACTIONS - 1).astype(jnp.int32)
    action_table = bell_draw(splits[5], (ACTIONS, D), 1.0, 6.0)
    norm_gain = jnp.clip(1.0 + 0.1 * jax.random.normal(splits[6], (D,), jnp.float32), 0.5, 1.5)
    routes_keys = jax.random.split(jax.random.fold_in(splits[7], 1), CLIPS * FRAMES * FTOK // FTOK)
    routes_turns = jax.random.permutation(jax.random.fold_in(splits[7], 3), CLIPS * FRAMES * FTOK // FTOK)
    routes = jax.vmap(lambda own, number: routed_block(jax.random.fold_in(splits[7], 2), own, number, FTOK, EXPERTS, TOPK, CAP, 2))(routes_keys, routes_turns).reshape((CLIPS, FRAMES, FTOK, TOPK))
    gate_probs = jnp.clip(jnp.exp(math.log(1.0) - 2.3025851 * jax.random.uniform(splits[8], (CLIPS, FRAMES, FTOK, TOPK), jnp.float32) ** block_scale(splits[8], (CLIPS, FRAMES, FTOK, TOPK), ((0, 4), (1, 8)), -0.2, 0.2)), 0.1, 1.0)
    predicted = with_ends((jax.random.randint(splits[9], (CLIPS, FRAMES, FTOK), 0, 2) < 1).astype(jnp.int32), jax.random.fold_in(splits[9], 1), 0, 1)
    cotangent = bell_draw(splits[10], (CLIPS, FRAMES, FTOK, D), 0.15, 0.8984375, ((0, 4), (1, 8)))
    up_weight = bell_draw(splits[11], (EXPERTS, D, FF), D ** -0.5, 0.125, ((0, 4),))
    down_weight = bell_draw(splits[12], (EXPERTS, FF, D), FF ** -0.5, 0.1875, ((0, 4),))
    return {"tokens": tokens, "queries": queries, "key_rows": key_rows, "values": values, "actions": actions, "action_table": action_table, "norm_gain": norm_gain, "routes": routes, "gate_probs": gate_probs, "predicted": predicted, "cotangent": cotangent, "up_weight": up_weight, "down_weight": down_weight}


norm_eps = 1e-06
gelu_coef = 0.7978845608028654

def gelu_value(preact):
    inner = gelu_coef * (preact + 0.044715 * preact * preact * preact)
    return 0.5 * preact * (1.0 + jnp.tanh(inner))

def gelu_slope(preact):
    tanh_inner = jnp.tanh(gelu_coef * (preact + 0.044715 * preact * preact * preact))
    return 0.5 * (1.0 + tanh_inner) + 0.5 * preact * (1.0 - tanh_inner * tanh_inner) * gelu_coef * (1.0 + 3.0 * 0.044715 * preact * preact)

def attend(triple):
    query_blk, key_blk, value_blk = triple
    key_span = FRAMES * FTOK
    query_f32 = query_blk.reshape(key_span, HEADS, HD).astype(jnp.float32)
    key_f32 = key_blk.reshape(key_span, HEADS, HD).astype(jnp.float32)
    value_f32 = value_blk.reshape(key_span, HEADS, HD).astype(jnp.float32)
    scores = jnp.einsum('qhd,khd->hqk', query_f32, key_f32) * HD ** (-0.5)
    frame_ids = jnp.arange(key_span, dtype=jnp.int32) // FTOK
    allowed = frame_ids[None, :] <= frame_ids[:, None]
    scores = jnp.where(allowed[None], scores, -1e+30)
    maximum = lax.optimization_barrier(jnp.max(scores, -1, keepdims=True))
    exponent = jnp.exp(scores - maximum)
    weights = (exponent / lax.optimization_barrier(jnp.sum(exponent, -1, keepdims=True))).astype(jnp.bfloat16)
    attention_out = jnp.einsum('hqk,khd->qhd', weights.astype(jnp.float32), value_f32)
    return attention_out.reshape(FRAMES, FTOK, D)

def reference(tokens, queries, key_rows, values, actions, action_table, norm_gain, routes, gate_probs, predicted, cotangent, up_weight, down_weight):
    block_count = CLIPS * FRAMES
    pair_count = FTOK * TOPK
    attended = lax.map(attend, (queries, key_rows, values))
    action_rows = action_table[actions].astype(jnp.float32)
    stream = (tokens.astype(jnp.float32) + attended + action_rows[:, :, None, :]).astype(jnp.bfloat16)
    stream = lax.optimization_barrier(stream)
    stream_f32 = stream.astype(jnp.float32)
    inv_rms = lax.rsqrt(lax.optimization_barrier(jnp.mean(stream_f32 * stream_f32, -1, keepdims=True)) + norm_eps)
    unit_rows = stream_f32 * inv_rms
    normed = (unit_rows * norm_gain).astype(jnp.bfloat16)
    flat_routes = routes.reshape(block_count, pair_count)
    expert_hits = (flat_routes[:, :, None] == jnp.arange(EXPERTS, dtype=jnp.int32)).astype(jnp.int32)
    earlier = jnp.cumsum(expert_hits, 1) - expert_hits
    slot_rank = lax.optimization_barrier(jnp.sum(earlier * expert_hits, -1))
    block_ids = jnp.arange(block_count, dtype=jnp.int32)
    clip_ids = block_ids // FRAMES
    frame_ids = block_ids % FRAMES
    position = ((flat_routes * FRAMES + frame_ids[:, None]) * CLIPS + clip_ids[:, None]) * CAP + slot_rank
    position = position.reshape(-1).astype(jnp.int32)
    rows_total = EXPERTS * FRAMES * CLIPS * CAP
    token_rows = jnp.repeat(normed.reshape(block_count * FTOK, D), TOPK, axis=0)
    forward_buf = jnp.zeros((rows_total, D), jnp.bfloat16).at[position].set(token_rows)
    upstream = cotangent.astype(jnp.float32) * predicted[..., None].astype(jnp.float32)
    gate_f32 = gate_probs.reshape(block_count * FTOK, TOPK)
    scaled = (gate_f32[:, :, None] * upstream.reshape(block_count * FTOK, 1, D)).astype(jnp.bfloat16)
    backward_buf = jnp.zeros((rows_total, D), jnp.bfloat16).at[position].set(scaled.reshape(block_count * pair_count, D))
    frame_rows = CLIPS * CAP

    def run_expert(inputs):
        slots_in, slots_grad, up_mat, down_mat = inputs
        preact = jnp.dot(slots_in, up_mat, preferred_element_type=jnp.float32)
        activated = gelu_value(preact).astype(jnp.bfloat16)
        expert_out = jnp.dot(activated, down_mat, preferred_element_type=jnp.float32).astype(jnp.bfloat16)
        grad_act = jnp.dot(slots_grad, down_mat.T, preferred_element_type=jnp.float32)
        grad_pre = (grad_act * gelu_slope(preact)).astype(jnp.bfloat16)
        grad_slots = jnp.dot(grad_pre, up_mat.T, preferred_element_type=jnp.float32).astype(jnp.bfloat16)
        up_part = jnp.einsum('fsd,fsk->fdk', slots_in.reshape(FRAMES, frame_rows, D).astype(jnp.float32), grad_pre.reshape(FRAMES, frame_rows, FF).astype(jnp.float32))
        down_part = jnp.einsum('fsk,fsd->fkd', activated.reshape(FRAMES, frame_rows, FF).astype(jnp.float32), slots_grad.reshape(FRAMES, frame_rows, D).astype(jnp.float32))
        up_part = lax.optimization_barrier(up_part.astype(jnp.bfloat16)).astype(jnp.float32)
        down_part = lax.optimization_barrier(down_part.astype(jnp.bfloat16)).astype(jnp.float32)
        return (expert_out, grad_slots, lax.optimization_barrier(jnp.sum(up_part, 0)).astype(jnp.bfloat16), lax.optimization_barrier(jnp.sum(down_part, 0)).astype(jnp.bfloat16))
    outs_buf, grads_buf, up_grad, down_grad = lax.map(run_expert, (forward_buf.reshape(EXPERTS, -1, D), backward_buf.reshape(EXPERTS, -1, D), up_weight, down_weight))
    outs_buf = lax.optimization_barrier(outs_buf)
    grads_buf = lax.optimization_barrier(grads_buf)
    picked = outs_buf.reshape(rows_total, D)[position].astype(jnp.float32).reshape(block_count * FTOK, TOPK, D)
    mixture = lax.optimization_barrier(jnp.sum(gate_f32[:, :, None] * picked, 1))
    layer_out = (stream_f32.reshape(-1, D) + mixture).astype(jnp.bfloat16).reshape(tokens.shape)
    norm_back = lax.optimization_barrier(jnp.sum(grads_buf.reshape(rows_total, D)[position].astype(jnp.float32).reshape(block_count * FTOK, TOPK, D), 1))
    scaled_back = norm_back * norm_gain
    unit_flat = unit_rows.reshape(-1, D)
    inv_flat = inv_rms.reshape(-1, 1)
    stream_grad = upstream.reshape(-1, D) + inv_flat * (scaled_back - unit_flat * lax.optimization_barrier(jnp.mean(scaled_back * unit_flat, -1, keepdims=True)))
    return (layer_out, stream_grad.astype(jnp.bfloat16).reshape(tokens.shape), up_grad, down_grad)
```

```python
import functools

import jax
import jax.numpy as jnp
from jax import lax
from jax.experimental import pallas as pl
from jax.experimental.pallas import tpu as pltpu
from jax.sharding import PartitionSpec as P

HEADS = 16
HD = 128
TOPK = 2
CORES = 2
CHUNKS = 2
NEG = -1e30


norm_eps = 1e-06
gelu_coef = 0.7978845608028654


def gelu_value(preact):
    inner = gelu_coef * (preact + 0.044715 * preact * preact * preact)
    return 0.5 * preact * (1.0 + jnp.tanh(inner))


def gelu_slope(preact):
    tanh_inner = jnp.tanh(gelu_coef * (preact + 0.044715 * preact * preact * preact))
    return 0.5 * (1.0 + tanh_inner) + 0.5 * preact * (1.0 - tanh_inner * tanh_inner) * gelu_coef * (
        1.0 + 3.0 * 0.044715 * preact * preact
    )


def attention_kernel(n_query, n_key, heads, bias_ref, *refs):
    query_refs = refs[:n_query]
    pair_refs = refs[n_query : n_query + n_key]
    out_refs = refs[n_query + n_key : 2 * n_query + n_key]
    stat_refs = refs[2 * n_query + n_key :]
    head = pl.program_id(0)
    rows = query_refs[0].shape[0]
    keys = jnp.concatenate([r[0] for r in pair_refs], axis=0)
    vals = jnp.concatenate([r[1] for r in pair_refs], axis=0)
    span = keys.shape[0] // n_key
    lane = lax.broadcasted_iota(jnp.int32, (rows, HD), 1)
    for q in range(n_query):
        scores = lax.dot_general(
            query_refs[q][...], keys, (((1,), (1,)), ((), ())), preferred_element_type=jnp.float32
        ) * HD ** (-0.5)
        scores = jnp.concatenate(
            [scores[:, k * span : (k + 1) * span] + bias_ref[q, k] for k in range(n_key)], axis=1
        )
        top = jnp.max(scores, axis=1, keepdims=True)
        weight = jnp.exp(scores - top)
        total = jnp.sum(weight, axis=1, keepdims=True)
        mixed = lax.dot_general(
            weight.astype(jnp.bfloat16), vals, (((1,), (0,)), ((), ())), preferred_element_type=jnp.float32
        )
        out_refs[q][:, pl.ds(pl.multiple_of(head * HD, HD), HD)] = (mixed / total).astype(jnp.bfloat16)
        level = top + jnp.log(total)
        held = jnp.where(head == 0, jnp.zeros((rows, HD), jnp.float32), stat_refs[q][...])
        stat_refs[q][...] = jnp.where(lane == head, level, held)

    @pl.when(head == heads - 1)
    def _():
        for q in range(n_query):
            level = stat_refs[q][...]
            coarse = level.astype(jnp.bfloat16)
            rest = level - coarse.astype(jnp.float32)
            middle = rest.astype(jnp.bfloat16)
            fine = (rest - middle.astype(jnp.float32)).astype(jnp.bfloat16)
            base = heads * HD
            out_refs[q][:, base : base + HD] = coarse
            out_refs[q][:, base + HD : base + 2 * HD] = middle
            out_refs[q][:, base + 2 * HD : base + 3 * HD] = fine


def partial_attention(queries, pairs, bias, heads):
    rows = queries[0].shape[0]
    n_query, n_key = len(queries), len(pairs)
    wide = (heads + 3) * HD
    return pl.pallas_call(
        functools.partial(attention_kernel, n_query, n_key, heads),
        grid=(heads,),
        in_specs=[pl.BlockSpec(memory_space=pltpu.SMEM)]
        + [pl.BlockSpec((rows, HD), lambda h: (0, h))] * n_query
        + [pl.BlockSpec((2, rows, HD), lambda h: (0, 0, h))] * n_key,
        out_specs=[pl.BlockSpec((rows, wide), lambda h: (0, 0))] * n_query,
        out_shape=[jax.ShapeDtypeStruct((rows, wide), jnp.bfloat16)] * n_query,
        scratch_shapes=[pltpu.VMEM((rows, HD), jnp.float32)] * n_query,
        name="partial_attention",
    )(bias, *queries, *pairs)


def merge_kernel(n_part, chunks, heads, valid_ref, *refs):
    part_refs = refs[: n_part * chunks]
    tokens_ref, action_ref, gain_ref, place_ref = refs[n_part * chunks : n_part * chunks + 4]
    stream_ref, inv_ref, slots_ref, acc_ref = refs[n_part * chunks + 4 :]
    base = heads * HD
    for chunk in range(chunks):
        parts = part_refs[chunk * n_part : (chunk + 1) * n_part]
        levels = []
        for i, ref in enumerate(parts):
            level = (
                ref[:, base : base + HD].astype(jnp.float32)
                + ref[:, base + HD : base + 2 * HD].astype(jnp.float32)
                + ref[:, base + 2 * HD : base + 3 * HD].astype(jnp.float32)
            )
            levels.append(jnp.where(valid_ref[i] > 0, level, NEG))
        top = functools.reduce(jnp.maximum, levels)
        shares = [jnp.exp(level - top) for level in levels]
        total = functools.reduce(jnp.add, shares)
        shares = [share / total for share in shares]
        for h in range(heads):
            mixed = None
            for share, ref in zip(shares, parts):
                term = share[:, h : h + 1] * ref[:, h * HD : (h + 1) * HD].astype(jnp.float32)
                mixed = term if mixed is None else mixed + term
            col = (chunk * heads + h) * HD
            row = tokens_ref[:, col : col + HD].astype(jnp.float32) + mixed + action_ref[:, col : col + HD]
            stream_ref[:, col : col + HD] = row.astype(jnp.bfloat16)
    stream = stream_ref[...].astype(jnp.float32)
    inv_rms = lax.rsqrt(jnp.mean(stream * stream, axis=1, keepdims=True) + norm_eps)
    inv_ref[...] = jnp.broadcast_to(inv_rms, inv_ref.shape)
    acc_ref[...] = (stream * inv_rms * gain_ref[...]).astype(jnp.bfloat16)
    slots = slots_ref.shape[0]
    slot = lax.broadcasted_iota(jnp.int32, (slots, place_ref.shape[1]), 0)
    chosen = (slot == place_ref[0:1, :]) | (slot == place_ref[1:2, :])
    slots_ref[...] = jnp.dot(
        chosen.astype(jnp.float32).astype(jnp.bfloat16), acc_ref[...], preferred_element_type=jnp.float32
    ).astype(jnp.bfloat16)


def merge(parts, valid, tokens, action_row, gain, place, slots, heads):
    rows, width = tokens.shape
    n_part, chunks = len(parts[0]), len(parts)
    flat = [p for chunk in parts for p in chunk]
    vmem = pl.BlockSpec(memory_space=pltpu.VMEM)
    return pl.pallas_call(
        functools.partial(merge_kernel, n_part, chunks, heads),
        in_specs=[pl.BlockSpec(memory_space=pltpu.SMEM)] + [vmem] * (len(flat) + 4),
        out_specs=[vmem] * 3,
        out_shape=[
            jax.ShapeDtypeStruct((rows, width), jnp.bfloat16),
            jax.ShapeDtypeStruct((rows, HD), jnp.float32),
            jax.ShapeDtypeStruct((slots, width), jnp.bfloat16),
        ],
        scratch_shapes=[pltpu.VMEM((rows, width), jnp.bfloat16)],
        name="merge_norm_dispatch",
    )(valid, *flat, tokens, action_row, gain, place)


def dot(a, b, dims):
    return lax.dot_general(a, b, (dims, ((), ())), preferred_element_type=jnp.float32)


def local(
    tokens,
    queries,
    key_rows,
    values,
    actions,
    action_table,
    norm_gain,
    routes,
    gate_probs,
    predicted,
    cotangent,
    up_weight,
    down_weight,
):
    shape = tokens.shape
    rows, width = shape[2], shape[3]
    lanes = lax.axis_size("tm")
    chips = lanes // CORES
    experts = lax.axis_size("expert")
    me = lax.axis_index("expert")
    chip = lax.axis_index("tm") // CORES
    core = lax.axis_index("tm") % CORES
    hidden = up_weight.shape[2]
    up_w, down_w = up_weight[0], down_weight[0]

    def across(x, pairs):
        return lax.ppermute(x, "tm", [(CORES * a + c, CORES * b + c) for a, b in pairs for c in range(CORES)])

    def swap(x, only=None):
        which = range(chips) if only is None else only
        return lax.ppermute(x, "tm", [(CORES * a + c, CORES * a + 1 - c) for a in which for c in range(CORES)])

    def exchange(blocks):
        return [blocks[0]] + [
            lax.ppermute(blocks[k], "expert", [(i, i ^ k) for i in range(experts)]) for k in range(1, experts)
        ]

    query = queries.reshape(rows, width)
    pair = jnp.concatenate([key_rows.reshape(1, rows, width), values.reshape(1, rows, width)], axis=0)
    heads = HEADS // CHUNKS
    hubs = [h for h in range(chips) if h % 2 == 1]
    guest_shifts = [s for s in range(1, chips) if any(h + s < chips for h in hubs)]
    pair_mate = swap(pair)
    piece = [slice(i * heads * HD, (i + 1) * heads * HD) for i in range(CHUNKS)]
    prev_own = [across(pair[:, :, p], [(h - 1, h) for h in hubs]) for p in piece]
    guests = [
        [across(query[:, p], [(h + s, h) for h in hubs if h + s < chips]) for s in guest_shifts] for p in piece
    ]
    is_hub = chip % 2 == 1
    zero = jnp.float32(0.0)
    prev_bias = jnp.where(is_hub, zero, NEG)
    mate_bias = jnp.where(core == 1, zero, NEG)
    home = partial_attention(
        [query], [pair, pair_mate], jnp.stack([zero, mate_bias]).reshape(1, 2), HEADS
    )[0]

    flat_routes = routes.reshape(-1)
    capacity = max(2, rows * TOPK * 5 // (4 * experts))
    slots = experts * capacity
    hits = (flat_routes[:, None] == lax.broadcasted_iota(jnp.int32, (1, experts), 1)).astype(jnp.int32)
    earlier = jnp.cumsum(hits, 0) - hits
    rank = jnp.sum(earlier * hits, 1)
    position = ((flat_routes ^ me) * capacity + rank).reshape(-1, TOPK)
    place = (position[:, :, None] == lax.broadcasted_iota(jnp.int32, (1, 1, slots), 2)).astype(jnp.bfloat16)
    gate = gate_probs.reshape(-1, TOPK)
    upstream = cotangent.astype(jnp.float32).reshape(-1, width) * predicted.reshape(-1, 1).astype(jnp.float32)
    scaled = (gate[:, :, None] * upstream[:, None, :]).astype(jnp.bfloat16)
    grad_send = jnp.einsum("tks,tkd->sd", place, scaled, preferred_element_type=jnp.float32).astype(jnp.bfloat16)
    grad_in = jnp.concatenate(
        exchange([grad_send[k * capacity : (k + 1) * capacity] for k in range(experts)]), axis=0
    )
    grad_mate = swap(grad_in)
    grad_act = dot(grad_in, down_w, ((1,), (1,)))
    action_row = jnp.dot(
        (actions.reshape(1, 1) == lax.broadcasted_iota(jnp.int32, (1, action_table.shape[0]), 1)).astype(jnp.bfloat16),
        action_table,
        preferred_element_type=jnp.float32,
    )

    guest_bias = jnp.zeros((len(guest_shifts), 2 * CORES), jnp.float32)
    own_bias = jnp.stack([prev_bias, prev_bias, jnp.float32(NEG), jnp.float32(NEG)]).reshape(1, 2 * CORES)
    bias = jnp.concatenate([own_bias, guest_bias], axis=0)
    parts = []
    for i, p in enumerate(piece):
        prev_mate = swap(prev_own[i], hubs)
        made = partial_attention(
            [query[:, p]] + guests[i],
            [prev_own[i], prev_mate, pair[:, :, p], pair_mate[:, :, p]],
            bias,
            heads,
        )
        back = [
            across(made[1 + j], [(h, h + s) for h in hubs if h + s < chips]) for j, s in enumerate(guest_shifts)
        ]
        base = HEADS * HD
        stats = jnp.concatenate(
            [
                jnp.pad(home[:, base + k * HD + i * heads : base + k * HD + (i + 1) * heads], ((0, 0), (0, HD - heads)))
                for k in range(3)
            ],
            axis=1,
        )
        mine = jnp.concatenate([home[:, p], stats], axis=1)
        parts.append([mine, made[0]] + back)
    valid = jnp.stack(
        [jnp.int32(1), is_hub.astype(jnp.int32)]
        + [((chip - s >= 1) & ((chip - s) % 2 == 1)).astype(jnp.int32) for s in guest_shifts]
    )
    stream, inv_wide, slots_out = merge(
        parts,
        valid,
        tokens.reshape(rows, width),
        action_row,
        norm_gain.reshape(1, width),
        position.T,
        slots,
        heads,
    )
    inv_rms = inv_wide[:, :1]

    received = jnp.concatenate(
        exchange([slots_out[k * capacity : (k + 1) * capacity] for k in range(experts)]), axis=0
    )

    def split(x, which):
        kept = x.reshape(x.shape[0], chips, CORES, -1)
        return lax.dynamic_index_in_dim(kept, which, 2, keepdims=False).reshape(x.shape[0], -1)

    received_mate = swap(split(received, 1 - core))
    preact = dot(received, up_w, ((1,), (0,)))
    activated = gelu_value(preact).astype(jnp.bfloat16)
    grad_pre = (grad_act * gelu_slope(preact)).astype(jnp.bfloat16)
    late = swap(jnp.concatenate([grad_pre, split(activated, 1 - core)], axis=1))
    grad_pre_mate, activated_mate = late[:, :hidden], late[:, hidden:]
    expert_out = dot(activated, down_w, ((1,), (0,))).astype(jnp.bfloat16)
    up_part = (
        dot(split(received, core), grad_pre, ((0,), (0,))) + dot(received_mate, grad_pre_mate, ((0,), (0,)))
    ).astype(jnp.bfloat16)
    down_part = (
        dot(split(activated, core), grad_in, ((0,), (0,))) + dot(activated_mate, grad_mate, ((0,), (0,)))
    ).astype(jnp.bfloat16)
    grad_slots = dot(grad_pre, up_w, ((1,), (1,))).astype(jnp.bfloat16)

    arrays = [up_part.reshape(chips, -1, hidden), down_part.reshape(chips, -1, width)]
    rising, falling = [None, None], [None, None]

    def take(x, which, more):
        own = lax.dynamic_index_in_dim(x, jnp.clip(which, 0, chips - 1), 0, keepdims=False)
        if more is None:
            return own
        return (own.astype(jnp.float32) + more.astype(jnp.float32)).astype(jnp.bfloat16)

    for step in range(1, chips):
        for i, x in enumerate(arrays):
            far = chips - step
            rising[i] = across(take(x, chip + far, rising[i]), [(a, a + 1) for a in range(step)])
            falling[i] = across(
                take(x, chip - far, falling[i]), [(chips - 1 - a, chips - 2 - a) for a in range(step)]
            )
    up_total, down_total = [
        (
            lax.dynamic_index_in_dim(x, chip, 0, keepdims=False).astype(jnp.float32)
            + rising[i].astype(jnp.float32)
            + falling[i].astype(jnp.float32)
        ).astype(jnp.bfloat16)
        for i, x in enumerate(arrays)
    ]

    returned = jnp.concatenate(exchange([expert_out[k * capacity : (k + 1) * capacity] for k in range(experts)]), axis=0)
    grad_home = jnp.concatenate(exchange([grad_slots[k * capacity : (k + 1) * capacity] for k in range(experts)]), axis=0)
    stream_f32 = stream.astype(jnp.float32)
    picked = jnp.einsum("tks,sd->tkd", place, returned, preferred_element_type=jnp.float32)
    mixture = jnp.sum(gate[:, :, None] * picked, 1)
    layer_out = (stream_f32 + mixture).astype(jnp.bfloat16).reshape(shape)
    norm_back = jnp.einsum("tks,sd->td", place, grad_home, preferred_element_type=jnp.float32)
    unit_rows = stream_f32 * inv_rms
    scaled_back = norm_back * norm_gain
    stream_grad = upstream + inv_rms * (
        scaled_back - unit_rows * jnp.mean(scaled_back * unit_rows, -1, keepdims=True)
    )
    return (
        layer_out,
        stream_grad.astype(jnp.bfloat16).reshape(shape),
        up_total[None],
        down_total[None],
    )


def solution(mesh):
    in_specs = (
        P("expert", "tm", None, None),
        P("expert", "tm", None, None),
        P("expert", "tm", None, None),
        P("expert", "tm", None, None),
        P("expert", "tm"),
        P(),
        P(),
        P("expert", "tm", None, None),
        P("expert", "tm", None, None),
        P("expert", "tm", None),
        P("expert", "tm", None, None),
        P("expert", None, None),
        P("expert", None, None),
    )
    out_specs = (
        P("expert", "tm", None, None),
        P("expert", "tm", None, None),
        P("expert", "tm", None),
        P("expert", "tm", None),
    )
    return jax.shard_map(local, mesh=mesh, in_specs=in_specs, out_specs=out_specs, check_vma=False)
```

```python
import functools

import jax
import jax.numpy as jnp
from jax import lax
from jax.experimental import pallas as pl
from jax.experimental.pallas import tpu as pltpu
from jax.sharding import PartitionSpec as P

HEADS = 16
HD = 128
TOPK = 2
CORES = 2
CHUNKS = 2
NEG = -1e30


norm_eps = 1e-06
gelu_coef = 0.7978845608028654


def gelu_value(preact):
    inner = gelu_coef * (preact + 0.044715 * preact * preact * preact)
    return 0.5 * preact * (1.0 + jnp.tanh(inner))


def gelu_slope(preact):
    tanh_inner = jnp.tanh(gelu_coef * (preact + 0.044715 * preact * preact * preact))
    return 0.5 * (1.0 + tanh_inner) + 0.5 * preact * (1.0 - tanh_inner * tanh_inner) * gelu_coef * (
        1.0 + 3.0 * 0.044715 * preact * preact
    )

LOG2E = 1.4426950408889634
SCORE_SCALE = HD ** (-0.5) * LOG2E
PACK = 16


def attend(keys, vals, queries, bias=None):
    scores = lax.dot_general(keys, queries, (((1,), (1,)), ((), ())), preferred_element_type=jnp.float32)
    if bias is not None:
        half = keys.shape[0] // 2
        scores = jnp.concatenate([scores[:half], scores[half:] + bias], axis=0)
    top = jnp.max(scores, axis=0, keepdims=True)
    weight = jnp.exp2((scores - top) * SCORE_SCALE)
    total = jnp.sum(weight, axis=0, keepdims=True)
    mixed = lax.dot_general(
        vals, weight.astype(jnp.bfloat16), (((0,), (0,)), ((), ())), preferred_element_type=jnp.float32
    )
    return mixed / total, top * SCORE_SCALE + jnp.log2(total)


def home_kernel(heads, bias_ref, query_ref, key_ref, value_ref, mate_ref, out_ref, level_ref):
    bias = bias_ref[0, 0]

    def one(head, carry):
        col = pl.ds(pl.multiple_of(head * HD, HD), HD)
        keys = jnp.concatenate([key_ref[:, col], mate_ref[0, :, col]], axis=0)
        vals = jnp.concatenate([value_ref[:, col], mate_ref[1, :, col]], axis=0)
        out, level = attend(keys, vals, query_ref[:, col], bias)
        out_ref[col, :] = out.astype(jnp.bfloat16)
        level_ref[pl.ds(head, 1), :] = level
        return carry

    lax.fori_loop(0, heads, one, 0, unroll=2)


def home_attention(query, keys, vals, mate, bias, heads):
    rows = query.shape[0]
    vmem = pl.BlockSpec(memory_space=pltpu.VMEM)
    return pl.pallas_call(
        functools.partial(home_kernel, heads),
        in_specs=[pl.BlockSpec(memory_space=pltpu.SMEM)] + [vmem] * 4,
        out_specs=[vmem] * 2,
        out_shape=[
            jax.ShapeDtypeStruct((heads * HD, rows), jnp.bfloat16),
            jax.ShapeDtypeStruct((heads, rows), jnp.float32),
        ],
        name="home_attention",
    )(bias, query, keys, vals, mate)


def hub_kernel(first, heads, n_guest, query_ref, key_ref, value_ref, mate_ref, prev_ref, prev_mate_ref, *refs):
    guest_refs = refs[:n_guest]
    out_ref, level_ref = refs[n_guest : n_guest + 2]
    pack_refs = refs[n_guest + 2 : 2 * n_guest + 2]
    hold_ref = refs[2 * n_guest + 2]
    rows = query_ref.shape[0]
    hold_ref[...] = jnp.zeros_like(hold_ref)

    def one(head, carry):
        near = pl.ds(pl.multiple_of(head * HD, HD), HD)
        full = pl.ds(pl.multiple_of((first + head) * HD, HD), HD)
        prev_keys = jnp.concatenate([prev_ref[0, :, near], prev_mate_ref[0, :, near]], axis=0)
        prev_vals = jnp.concatenate([prev_ref[1, :, near], prev_mate_ref[1, :, near]], axis=0)
        keys = jnp.concatenate([prev_keys, key_ref[:, full], mate_ref[0, :, full]], axis=0)
        vals = jnp.concatenate([prev_vals, value_ref[:, full], mate_ref[1, :, full]], axis=0)
        out, level = attend(keys, vals, jnp.concatenate([g[:, near] for g in guest_refs], axis=0))
        for g in range(n_guest):
            pack_refs[g][near, :] = out[:, g * rows : (g + 1) * rows].astype(jnp.bfloat16)
            hold_ref[g, pl.ds(head, 1), :] = level[:, g * rows : (g + 1) * rows]
        out, level = attend(prev_keys, prev_vals, query_ref[:, full])
        out_ref[near, :] = out.astype(jnp.bfloat16)
        level_ref[pl.ds(head, 1), :] = level
        return carry

    lax.fori_loop(0, heads, one, 0, unroll=2)
    base = heads * HD
    for g in range(n_guest):
        level = hold_ref[g]
        coarse = level.astype(jnp.bfloat16)
        rest = level - coarse.astype(jnp.float32)
        middle = rest.astype(jnp.bfloat16)
        fine = (rest - middle.astype(jnp.float32)).astype(jnp.bfloat16)
        for i, piece in enumerate((coarse, middle, fine)):
            pack_refs[g][base + i * PACK : base + (i + 1) * PACK, :] = piece


def hub_attention(query, keys, vals, mate, prev, prev_mate, guests, first, heads):
    rows = query.shape[0]
    vmem = pl.BlockSpec(memory_space=pltpu.VMEM)
    made = pl.pallas_call(
        functools.partial(hub_kernel, first, heads, len(guests)),
        in_specs=[vmem] * (6 + len(guests)),
        out_specs=[vmem] * (2 + len(guests)),
        out_shape=[
            jax.ShapeDtypeStruct((heads * HD, rows), jnp.bfloat16),
            jax.ShapeDtypeStruct((heads, rows), jnp.float32),
        ]
        + [jax.ShapeDtypeStruct((heads * HD + 3 * PACK, rows), jnp.bfloat16)] * len(guests),
        scratch_shapes=[pltpu.VMEM((len(guests), PACK, rows), jnp.float32)],
        name="hub_attention",
    )(query, keys, vals, mate, prev, prev_mate, *guests)
    return made[0], made[1], made[2:]


def merge_kernel(chunks, heads, n_back, experts, capacity, valid_ref, *refs):
    per = 2 + n_back
    home_ref, home_level_ref = refs[:2]
    chunk_refs = [refs[2 + i * per : 2 + (i + 1) * per] for i in range(chunks)]
    at = 2 + chunks * per
    base_ref, gain_ref, place_ref = refs[at : at + 3]
    stream_ref = refs[at + 3]
    slot_refs = refs[at + 4 : at + 4 + experts]
    share_ref, normed_ref = refs[at + 4 + experts :]
    groups = (n_back + 1) // 2
    width = base_ref.shape[0]
    squares = jnp.zeros((1, base_ref.shape[1]), jnp.float32)
    for chunk in range(chunks):
        own_ref, own_level_ref = chunk_refs[chunk][:2]
        back_refs = chunk_refs[chunk][2:]
        pairs = [back_refs[2 * i : 2 * i + 2] for i in range(groups)]
        levels = [
            home_level_ref[chunk * heads : (chunk + 1) * heads, :],
            jnp.where(valid_ref[0] > 0, own_level_ref[...], NEG),
        ]
        for i, pair in enumerate(pairs):
            level = jnp.zeros((PACK, base_ref.shape[1]), jnp.float32)
            for ref in pair:
                for j in range(3):
                    level = level + ref[heads * HD + j * PACK : heads * HD + (j + 1) * PACK, :].astype(jnp.float32)
            levels.append(jnp.where(valid_ref[1 + i] > 0, level[:heads], NEG))
        top = functools.reduce(jnp.maximum, levels)
        shares = [jnp.exp2(level - top) for level in levels]
        total = functools.reduce(jnp.add, shares)
        for i, share in enumerate(shares):
            share_ref[i, chunk * heads : (chunk + 1) * heads, :] = share / total

        def one(head, squares, chunk=chunk, own_ref=own_ref, pairs=pairs):
            near = pl.ds(pl.multiple_of(head * HD, HD), HD)
            full = pl.ds(pl.multiple_of((chunk * heads + head) * HD, HD), HD)
            at_head = pl.ds(chunk * heads + head, 1)
            row = base_ref[full, :] + share_ref[0, at_head, :] * home_ref[full, :].astype(jnp.float32)
            row = row + share_ref[1, at_head, :] * own_ref[near, :].astype(jnp.float32)
            for i, pair in enumerate(pairs):
                part = functools.reduce(jnp.add, [ref[near, :].astype(jnp.float32) for ref in pair])
                row = row + share_ref[2 + i, at_head, :] * part
            row = row.astype(jnp.bfloat16)
            stream_ref[full, :] = row
            row = row.astype(jnp.float32)
            return squares + jnp.sum(row * row, axis=0, keepdims=True)

        squares = lax.fori_loop(0, heads, one, squares, unroll=2)
    inv_rms = lax.rsqrt(squares / width + norm_eps)

    def scale(i, carry):
        full = pl.ds(pl.multiple_of(i * HD, HD), HD)
        normed_ref[full, :] = (stream_ref[full, :].astype(jnp.float32) * inv_rms * gain_ref[full, :]).astype(jnp.bfloat16)
        return carry

    lax.fori_loop(0, width // HD, scale, 0, unroll=2)
    slot = lax.broadcasted_iota(jnp.int32, (capacity, place_ref.shape[1]), 0)
    tile = min(width, 512)
    for k in range(experts):
        chosen = (slot + k * capacity == place_ref[0:1, :]) | (slot + k * capacity == place_ref[1:2, :])
        chosen = jnp.where(chosen, 1.0, 0.0).astype(jnp.bfloat16)
        for j in range(width // tile):
            slot_refs[k][:, j * tile : (j + 1) * tile] = lax.dot_general(
                chosen,
                normed_ref[j * tile : (j + 1) * tile, :],
                (((1,), (1,)), ((), ())),
                preferred_element_type=jnp.float32,
            ).astype(jnp.bfloat16)


def merge(home, parts, valid, base, gain, place, experts, capacity, heads):
    width, rows = base.shape
    n_back = len(parts[0]) - 2
    flat = [p for chunk in parts for p in chunk]
    vmem = pl.BlockSpec(memory_space=pltpu.VMEM)
    made = pl.pallas_call(
        functools.partial(merge_kernel, len(parts), heads, n_back, experts, capacity),
        in_specs=[pl.BlockSpec(memory_space=pltpu.SMEM)] + [vmem] * (2 + len(flat) + 3),
        out_specs=[vmem] * (1 + experts),
        out_shape=[jax.ShapeDtypeStruct((width, rows), jnp.bfloat16)]
        + [jax.ShapeDtypeStruct((capacity, width), jnp.bfloat16)] * experts,
        scratch_shapes=[
            pltpu.VMEM((2 + (n_back + 1) // 2, heads * len(parts), rows), jnp.float32),
            pltpu.VMEM((width, rows), jnp.bfloat16),
        ],
        name="merge_norm_dispatch",
    )(valid, *home, *flat, base, gain, place)
    return made[0], made[1:]


def expert_kernel(chips, n_block, core_ref, *refs):
    block_refs = refs[:n_block]
    weight_ref, grad_ref = refs[n_block : n_block + 2]
    act_ref, pre_ref, act_own_ref, rows_own_ref, late_ref, rows_ref = refs[n_block + 2 :]
    step = pl.program_id(0)
    core = core_ref[0]
    hidden = pre_ref.shape[1] * chips
    size = pre_ref.shape[1] // CORES
    width = rows_ref.shape[1]
    shard = width // (chips * CORES)

    @pl.when(step == 0)
    def _():
        at = 0
        for ref in block_refs:
            rows_ref[at : at + ref.shape[0], :] = ref[...]
            at += ref.shape[0]
        for chip in range(chips):
            mine = pl.ds(pl.multiple_of((chip * CORES + core) * shard, shard), shard)
            others = pl.ds(pl.multiple_of((chip * CORES + 1 - core) * shard, shard), shard)
            rows_own_ref[:, chip * shard : (chip + 1) * shard] = rows_ref[:, mine]
            at = hidden + hidden // CORES + chip * shard
            late_ref[:, at : at + shard] = rows_ref[:, others]

    preact = jnp.dot(rows_ref[...], weight_ref[...], preferred_element_type=jnp.float32)
    inner = jnp.tanh(gelu_coef * (preact + 0.044715 * preact * preact * preact))
    act = (0.5 * preact * (1.0 + inner)).astype(jnp.bfloat16)
    slope = 0.5 * (1.0 + inner) + 0.5 * preact * (1.0 - inner * inner) * gelu_coef * (
        1.0 + 3.0 * 0.044715 * preact * preact
    )
    pre = (grad_ref[...] * slope).astype(jnp.bfloat16)
    act_ref[...] = act
    pre_ref[...] = pre
    act_own_ref[...] = jnp.where(core == 0, act[:, :size], act[:, size:])
    late_ref[:, pl.ds(pl.multiple_of(step * CORES * size, CORES * size), CORES * size)] = pre
    late_ref[:, pl.ds(pl.multiple_of(hidden + step * size, size), size)] = jnp.where(
        core == 0, act[:, size:], act[:, :size]
    )


def expert_stage(blocks, weight, grad_act, core, chips):
    width, hidden = weight.shape
    total = grad_act.shape[0]
    tile = hidden // chips
    return pl.pallas_call(
        functools.partial(expert_kernel, chips, len(blocks)),
        grid=(chips,),
        in_specs=[pl.BlockSpec(memory_space=pltpu.SMEM)]
        + [pl.BlockSpec(b.shape, lambda j: (0, 0)) for b in blocks]
        + [pl.BlockSpec((width, tile), lambda j: (0, j)), pl.BlockSpec((total, tile), lambda j: (0, j))],
        out_specs=[
            pl.BlockSpec((total, tile), lambda j: (0, j)),
            pl.BlockSpec((total, tile), lambda j: (0, j)),
            pl.BlockSpec((total, tile // CORES), lambda j: (0, j)),
            pl.BlockSpec((total, width // CORES), lambda j: (0, 0)),
            pl.BlockSpec((total, hidden + hidden // CORES + width // CORES), lambda j: (0, 0)),
        ],
        out_shape=[
            jax.ShapeDtypeStruct((total, hidden), jnp.bfloat16),
            jax.ShapeDtypeStruct((total, hidden), jnp.bfloat16),
            jax.ShapeDtypeStruct((total, hidden // CORES), jnp.bfloat16),
            jax.ShapeDtypeStruct((total, width // CORES), jnp.bfloat16),
            jax.ShapeDtypeStruct((total, hidden + hidden // CORES + width // CORES), jnp.bfloat16),
        ],
        scratch_shapes=[pltpu.VMEM((total, width), jnp.bfloat16)],
        name="expert_stage",
    )(core, *blocks, weight, grad_act)


def weight_grad_kernel(left_ref, left_mate_ref, right_ref, right_mate_ref, out_ref):
    dims = (((0,), (0,)), ((), ()))
    total = lax.dot_general(left_ref[...], right_ref[...], dims, preferred_element_type=jnp.float32)
    total = total + lax.dot_general(left_mate_ref[...], right_mate_ref[...], dims, preferred_element_type=jnp.float32)
    out_ref[0] = total.astype(jnp.bfloat16)


def weight_grad(left, left_mate, left_at, right, right_mate, chips, name):
    total, cols = left.shape
    shard, wide = cols // chips, right.shape[1]
    at = left_at // shard
    return pl.pallas_call(
        weight_grad_kernel,
        grid=(chips,),
        in_specs=[
            pl.BlockSpec((total, shard), lambda j: (0, j)),
            pl.BlockSpec((total, shard), lambda j: (0, at + j)),
            pl.BlockSpec((total, wide), lambda j: (0, 0)),
            pl.BlockSpec((total, wide), lambda j: (0, 0)),
        ],
        out_specs=pl.BlockSpec((1, shard, wide), lambda j: (j, 0, 0)),
        out_shape=jax.ShapeDtypeStruct((chips, shard, wide), jnp.bfloat16),
        name=name,
    )(left, left_mate, right, right_mate)


def dot(a, b, dims):
    return lax.dot_general(a, b, (dims, ((), ())), preferred_element_type=jnp.float32)


def local(
    tokens,
    queries,
    key_rows,
    values,
    actions,
    action_table,
    norm_gain,
    routes,
    gate_probs,
    predicted,
    cotangent,
    up_weight,
    down_weight,
):
    shape = tokens.shape
    rows, width = shape[2], shape[3]
    lanes = lax.axis_size("tm")
    chips = lanes // CORES
    experts = lax.axis_size("expert")
    me = lax.axis_index("expert")
    chip = lax.axis_index("tm") // CORES
    core = lax.axis_index("tm") % CORES
    hidden = up_weight.shape[2]
    up_w, down_w = up_weight[0], down_weight[0]

    def across(x, pairs):
        return lax.ppermute(x, "tm", [(CORES * a + c, CORES * b + c) for a, b in pairs for c in range(CORES)])

    def swap(x, only=None):
        which = range(chips) if only is None else only
        return lax.ppermute(x, "tm", [(CORES * a + c, CORES * a + 1 - c) for a in which for c in range(CORES)])

    def exchange(blocks):
        return [blocks[0]] + [
            lax.ppermute(blocks[k], "expert", [(i, i ^ k) for i in range(experts)]) for k in range(1, experts)
        ]

    query, keys, vals = (x.reshape(rows, width) for x in (queries, key_rows, values))
    heads = HEADS // CHUNKS
    part = heads * HD
    hubs = [h for h in range(chips) if h % 2 == 1]
    shifts = [s for s in range(1, chips) if any(h + s < chips for h in hubs)]

    def send_chunk(i, query, keys, vals):
        cols = slice(i * part, (i + 1) * part)
        both = jnp.stack([keys[:, cols], vals[:, cols]])
        prev = across(both, [(h - 1, h) for h in hubs])
        asked = query[:, cols]
        return prev, [across(asked, [(h + s, h) for h in hubs if h + s < chips]) for s in shifts]

    pair_mate = swap(jnp.stack([keys, vals]))
    sent = [send_chunk(0, query, keys, vals)]
    is_hub = chip % 2 == 1
    mate_bias = jnp.where(core == 1, jnp.float32(0.0), NEG).reshape(1, 1)
    home = home_attention(query, keys, vals, pair_mate, mate_bias, HEADS)
    for i in range(1, CHUNKS):
        held = lax.optimization_barrier((query, keys, vals, home[1]))
        sent.append(send_chunk(i, *held[:3]))

    flat_routes = routes.reshape(-1)
    capacity = max(2, rows * TOPK * 5 // (4 * experts))
    slots = experts * capacity
    hits = (flat_routes[:, None] == lax.broadcasted_iota(jnp.int32, (1, experts), 1)).astype(jnp.int32)
    earlier = jnp.cumsum(hits, 0) - hits
    rank = jnp.sum(earlier * hits, 1)
    position = ((flat_routes ^ me) * capacity + rank).reshape(-1, TOPK)
    place = (position[:, :, None] == lax.broadcasted_iota(jnp.int32, (1, 1, slots), 2)).astype(jnp.bfloat16)
    gate = gate_probs.reshape(-1, TOPK)
    upstream = cotangent.astype(jnp.float32).reshape(-1, width) * predicted.reshape(-1, 1).astype(jnp.float32)
    scaled = (gate[:, :, None] * upstream[:, None, :]).astype(jnp.bfloat16)
    grad_send = jnp.einsum("tks,tkd->sd", place, scaled, preferred_element_type=jnp.float32).astype(jnp.bfloat16)
    grad_in = jnp.concatenate(
        exchange([grad_send[k * capacity : (k + 1) * capacity] for k in range(experts)]), axis=0
    )
    grad_mate = swap(grad_in)
    grad_act = dot(grad_in, down_w, ((1,), (1,)))
    action_row = jnp.dot(
        (actions.reshape(1, 1) == lax.broadcasted_iota(jnp.int32, (1, action_table.shape[0]), 1)).astype(jnp.bfloat16),
        action_table,
        preferred_element_type=jnp.float32,
    )
    base = (tokens.reshape(rows, width).astype(jnp.float32) + action_row).T
    gain_wide = jnp.broadcast_to(norm_gain[:, None], (width, rows))

    parts = []
    for i in range(CHUNKS):
        prev, guests = sent[i]
        out, level, packs = hub_attention(
            query, keys, vals, pair_mate, prev, swap(prev, hubs), guests, i * heads, heads
        )
        back = [across(packs[j], [(h, h + s) for h in hubs if h + s < chips]) for j, s in enumerate(shifts)]
        parts.append([out, level] + back)
    served = [
        functools.reduce(
            jnp.logical_or, [(chip - s >= 1) & ((chip - s) % 2 == 1) for s in shifts[2 * g : 2 * g + 2]]
        )
        for g in range((len(shifts) + 1) // 2)
    ]
    valid = jnp.stack([is_hub] + served).astype(jnp.int32)
    stream_t, outgoing = merge(
        home, parts, valid, base, gain_wide, position.T, experts, capacity, heads
    )

    blocks = exchange(outgoing)
    if capacity % PACK:
        blocks = [jnp.concatenate(blocks, axis=0)]
    if (hidden // lanes) % HD == 0 and (width // lanes) % HD == 0:
        activated, grad_pre, act_own, rows_own, late = expert_stage(blocks, up_w, grad_act, core.reshape(1), chips)
        late = swap(late)
        expert_out = dot(activated, down_w, ((1,), (0,))).astype(jnp.bfloat16)
        act_at, rows_at = hidden, hidden + hidden // CORES
        up_part = weight_grad(rows_own, late, rows_at, grad_pre, late, chips, "up_grad")
        down_part = weight_grad(act_own, late, act_at, grad_in, grad_mate, chips, "down_grad")
    else:

        def split(x, which):
            kept = x.reshape(x.shape[0], chips, CORES, -1)
            return lax.dynamic_index_in_dim(kept, which, 2, keepdims=False).reshape(x.shape[0], -1)

        received = jnp.concatenate(blocks, axis=0)
        received_mate = swap(split(received, 1 - core))
        preact = dot(received, up_w, ((1,), (0,)))
        activated = gelu_value(preact).astype(jnp.bfloat16)
        grad_pre = (grad_act * gelu_slope(preact)).astype(jnp.bfloat16)
        late = swap(jnp.concatenate([grad_pre, split(activated, 1 - core)], axis=1))
        grad_pre_mate, activated_mate = late[:, :hidden], late[:, hidden:]
        expert_out = dot(activated, down_w, ((1,), (0,))).astype(jnp.bfloat16)
        up_part = (
            dot(split(received, core), grad_pre, ((0,), (0,))) + dot(received_mate, grad_pre_mate, ((0,), (0,)))
        ).astype(jnp.bfloat16)
        down_part = (
            dot(split(activated, core), grad_in, ((0,), (0,))) + dot(activated_mate, grad_mate, ((0,), (0,)))
        ).astype(jnp.bfloat16)
    grad_slots = dot(grad_pre, up_w, ((1,), (1,))).astype(jnp.bfloat16)

    arrays = [up_part.reshape(chips, -1, hidden), down_part.reshape(chips, -1, width)]
    rising, falling = [None, None], [None, None]

    def take(x, which, more):
        own = lax.dynamic_index_in_dim(x, jnp.clip(which, 0, chips - 1), 0, keepdims=False)
        if more is None:
            return own
        return (own.astype(jnp.float32) + more.astype(jnp.float32)).astype(jnp.bfloat16)

    for step in range(1, chips):
        for i, x in enumerate(arrays):
            far = chips - step
            rising[i] = across(take(x, chip + far, rising[i]), [(a, a + 1) for a in range(step)])
            falling[i] = across(
                take(x, chip - far, falling[i]), [(chips - 1 - a, chips - 2 - a) for a in range(step)]
            )
    up_total, down_total = [
        (
            lax.dynamic_index_in_dim(x, chip, 0, keepdims=False).astype(jnp.float32)
            + rising[i].astype(jnp.float32)
            + falling[i].astype(jnp.float32)
        ).astype(jnp.bfloat16)
        for i, x in enumerate(arrays)
    ]

    returned = jnp.concatenate(exchange([expert_out[k * capacity : (k + 1) * capacity] for k in range(experts)]), axis=0)
    grad_home = jnp.concatenate(exchange([grad_slots[k * capacity : (k + 1) * capacity] for k in range(experts)]), axis=0)
    stream_f32 = stream_t.T.astype(jnp.float32)
    inv_rms = lax.rsqrt(jnp.mean(stream_f32 * stream_f32, -1, keepdims=True) + norm_eps)
    picked = jnp.einsum("tks,sd->tkd", place, returned, preferred_element_type=jnp.float32)
    mixture = jnp.sum(gate[:, :, None] * picked, 1)
    layer_out = (stream_f32 + mixture).astype(jnp.bfloat16).reshape(shape)
    norm_back = jnp.einsum("tks,sd->td", place, grad_home, preferred_element_type=jnp.float32)
    unit_rows = stream_f32 * inv_rms
    scaled_back = norm_back * norm_gain
    stream_grad = upstream + inv_rms * (
        scaled_back - unit_rows * jnp.mean(scaled_back * unit_rows, -1, keepdims=True)
    )
    return (
        layer_out,
        stream_grad.astype(jnp.bfloat16).reshape(shape),
        up_total[None],
        down_total[None],
    )


def solution(mesh):
    in_specs = (
        P("expert", "tm", None, None),
        P("expert", "tm", None, None),
        P("expert", "tm", None, None),
        P("expert", "tm", None, None),
        P("expert", "tm"),
        P(),
        P(),
        P("expert", "tm", None, None),
        P("expert", "tm", None, None),
        P("expert", "tm", None),
        P("expert", "tm", None, None),
        P("expert", None, None),
        P("expert", None, None),
    )
    out_specs = (
        P("expert", "tm", None, None),
        P("expert", "tm", None, None),
        P("expert", "tm", None),
        P("expert", "tm", None),
    )
    return jax.shard_map(local, mesh=mesh, in_specs=in_specs, out_specs=out_specs, check_vma=False)
```
